32 devices in a mesh: ctx: 8 (over z, x), bulk: 4 (over y, core).
Axes of the slice: x: 2, y: 2, z: 4, core: 2. Of those that a mesh axis runs over, the one named last changes fastest.
Arguments:
- query: bfloat16 [8192, 5120], P(('ctx', 'bulk')), may hold values from -1 to 1
- keys: bfloat16 [8192, 1024], P(('ctx', 'bulk')), may hold values from -1 to 1
- values: bfloat16 [8192, 1024], P(('ctx', 'bulk')), may hold values from -6 to 6
- output: bfloat16 [8192, 5120], P(('ctx', 'bulk')), may hold values from -3 to 3
- grad_out: bfloat16 [8192, 5120], P(('ctx', 'bulk')), may hold values from -12 to 12
- logsumexp: float32 [8192, 40], P(('ctx', 'bulk')), may hold values from 3 to 5
- selected: int32 [64, 8, 3], P(('ctx', 'bulk')), may hold values from -1 to 63, as said below
Outputs:
- grad_query: bfloat16 [8192, 5120], P(('ctx', 'bulk'))
- grad_keys: bfloat16 [8192, 1024], P(('ctx', 'bulk'))
- grad_values: bfloat16 [8192, 1024], P(('ctx', 'bulk'))
The draws below stay inside these ranges and needn't reach their ends.
Inputs may be any that keep to these rules, and one draw needn't show every extreme that they name: `selected`: entry [b, h, s] is -1 (no block) or a block on a device before the device of block b. Over all entries of one device's 2 blocks, each other device is named at most once; a device with 48 or more devices before it has no -1. Every device but the first names the device just before it, and the last device names the first device.
All inputs are finite; a program needn't handle non-finite values.
Results may differ from the reference program's by a relative error of at most 0.0062.
Values may be sent and summed in bfloat16 or wider, within the bound.
No kernel may reach another device: no remote copies, remote signals or barrier semaphores. Data moves between devices by JAX's collectives and lax.ppermute only.
A program may use at most 192 MiB of HBM per device.

```python
import jax
import jax.numpy as jnp
from jax import lax

HD = 128
KVH = 8
GROUP = 5
QH = 40
BLK = 128
TOPK = 3
BPD = 2
TOKENS = 8192
BLOCKS = 64
DEVICES = 32


def draw_selected(key, part):
    count_peers = DEVICES
    per_device = BPD * KVH * TOPK
    width = count_peers + per_device
    first, second, third, fourth = jax.random.split(jax.random.fold_in(key, 17), 4)
    noise = jax.random.randint(first, (count_peers, width), 0, 65536)
    favour = jax.random.randint(second, (width,), 0, 4)
    columns = jnp.arange(width, dtype=jnp.int32)
    device_ids = jnp.arange(count_peers, dtype=jnp.int32)[:, None]
    base = (noise + favour[None, :] * 32768) * width + columns[None, :]
    forced = (columns[None, :] == device_ids - 1) | (columns[None, :] == 0) & (device_ids == count_peers - 1)
    base = jnp.where(forced, 1073741824 + columns[None, :], base)
    score = jnp.where(columns[None, :] < device_ids, base, -1 - columns[None, :])
    _, picked = lax.top_k(score, per_device)
    ranks = jnp.arange(per_device, dtype=jnp.int32)[None, :]
    usable = ranks < jnp.minimum(device_ids, per_device)
    order_keys = jax.random.randint(third, (count_peers, per_device), 0, 65536) * per_device + ranks
    shuffle = jnp.argsort(order_keys, axis=1)
    owners = jnp.take_along_axis(picked, shuffle, axis=1)
    usable = jnp.take_along_axis(usable, shuffle, axis=1)
    within = jax.random.randint(fourth, (count_peers, per_device), 0, BPD)
    chosen = jnp.where(usable, owners * BPD + within, -1)
    return chosen.reshape(count_peers * BPD, KVH, TOPK).astype(jnp.int32)


def levels(own_key, extent, cuts, least, top_value):
    gain, own = 1.0, jax.random.fold_in(own_key, 6)
    for axis_at, shards_of in cuts:
        heights = jnp.exp(jax.random.uniform(jax.random.fold_in(own, axis_at), (shards_of,), jnp.float32, least / len(cuts), top_value / len(cuts)))
        gain = gain * jnp.repeat(heights, extent[axis_at] // shards_of).reshape([-1 if axis == axis_at else 1 for axis in range(len(extent))])
    return gain


def normal_values(rng, extent, spread, reach, cuts=(), held_as=jnp.bfloat16):
    array = jax.random.normal(rng, extent, jnp.float32) * spread
    if len(cuts) > 0:
        array = levels(rng, extent, cuts, -0.22, 0.18) * array
    return jnp.clip(array, min=-reach, max=reach).astype(held_as)


def setup_inputs(seed: int = 0) -> dict:
    arg_keys = jax.random.split(jax.random.key(seed), 8)
    query = jnp.clip(jax.random.uniform(arg_keys[0], (TOKENS, QH * HD), jnp.float32, -1.0, 1.0) * levels(arg_keys[0], (TOKENS, QH * HD), ((0, 32),), -0.4, 0.0), -1.0, 1.0).astype(jnp.bfloat16)
    keys = jnp.clip(jax.random.uniform(arg_keys[1], (TOKENS, KVH * HD), jnp.float32, -1.0, 1.0) * levels(arg_keys[1], (TOKENS, KVH * HD), ((0, 32),), -0.4, 0.0), -1.0, 1.0).astype(jnp.bfloat16)
    values = normal_values(arg_keys[2], (TOKENS, KVH * HD), 1.0, 6.0, ((0, 32),))
    output = normal_values(arg_keys[3], (TOKENS, QH * HD), 0.5, 3.0, ((0, 32),))
    grad_out = normal_values(arg_keys[4], (TOKENS, QH * HD), 2.0, 12.0, ((0, 32),))
    logsumexp = jnp.clip(3.0 + 2.0 * jax.random.uniform(arg_keys[5], (TOKENS, QH), jnp.float32) ** levels(arg_keys[5], (TOKENS, QH), ((0, 32),), -0.2, 0.2), 3.0, 5.0)
    selected = draw_selected(jax.random.fold_in(arg_keys[7], 71), 0)
    return dict(query=query, keys=keys, values=values, output=output, grad_out=grad_out, logsumexp=logsumexp, selected=selected)


def reference(query, keys, values, output, grad_out, logsumexp, selected):
    scale = HD ** -0.5
    high = lax.Precision.HIGHEST
    query_blocks = query.reshape(BLOCKS, BLK, KVH, GROUP, HD)
    grad_blocks = grad_out.reshape(BLOCKS, BLK, KVH, GROUP, HD)
    key_blocks = keys.reshape(BLOCKS, BLK, KVH, HD)
    value_blocks = values.reshape(BLOCKS, BLK, KVH, HD)
    delta = jnp.sum(grad_out.astype(jnp.float32).reshape(TOKENS, KVH, GROUP, HD)
                    * output.astype(jnp.float32).reshape(TOKENS, KVH, GROUP, HD), axis=-1)
    delta = delta.reshape(BLOCKS, BLK, KVH, GROUP)
    stats = logsumexp.reshape(BLOCKS, BLK, KVH, GROUP)
    heads = jnp.arange(KVH, dtype=jnp.int32)
    positions = jnp.arange(BLK, dtype=jnp.int32)
    causal = positions[None, :] <= positions[:, None]
    slot_ids = jnp.arange(TOPK + 1, dtype=jnp.int32)
    allowed = (slot_ids[None, :, None] > 0) | causal[:, None, :]

    def step(carry, index):
        key_acc, value_acc = carry
        chosen = jnp.concatenate([jnp.full((KVH, 1), index, jnp.int32), selected[index].astype(jnp.int32)], axis=1)
        usable = chosen >= 0
        safe = jnp.maximum(chosen, 0).astype(jnp.int32)
        key_set = key_blocks[safe, :, heads[:, None], :].astype(jnp.float32)
        value_set = value_blocks[safe, :, heads[:, None], :].astype(jnp.float32)
        queries = query_blocks[index].astype(jnp.float32)
        grads = grad_blocks[index].astype(jnp.float32)
        scores = jnp.einsum('qhgd,hjkd->hgqjk', queries, key_set, precision=high) * scale
        mask = usable[:, None, None, :, None] & allowed[None, None]
        logs = jnp.transpose(stats[index], (1, 2, 0))[..., None, None]
        probs32 = jnp.where(mask, jnp.exp(scores - logs), 0.0)
        probs = lax.optimization_barrier(probs32.astype(jnp.bfloat16)).astype(jnp.float32)
        value_part = jnp.einsum('hgqjk,qhgd->hjkd', probs, grads, precision=high)
        dprobs = jnp.einsum('qhgd,hjkd->hgqjk', grads, value_set, precision=high)
        shift = jnp.transpose(delta[index], (1, 2, 0))[..., None, None]
        dscores = lax.optimization_barrier((probs32 * (dprobs - shift)).astype(jnp.bfloat16)).astype(jnp.float32)
        query_grad = jnp.einsum('hgqjk,hjkd->qhgd', dscores, key_set, precision=high) * scale
        key_part = jnp.einsum('hgqjk,qhgd->hjkd', dscores, queries, precision=high) * scale
        key_acc = key_acc.at[safe, :, heads[:, None], :].add(key_part)
        value_acc = value_acc.at[safe, :, heads[:, None], :].add(value_part)
        return (key_acc, value_acc), query_grad.astype(jnp.bfloat16).reshape(BLK, KVH * GROUP * HD)

    zeros = jnp.zeros((BLOCKS, BLK, KVH, HD), jnp.float32)
    (key_acc, value_acc), query_grads = lax.scan(step, (zeros, zeros), jnp.arange(BLOCKS, dtype=jnp.int32))
    grad_query = query_grads.reshape(TOKENS, KVH * GROUP * HD)
    grad_keys = key_acc.reshape(TOKENS, KVH * HD).astype(jnp.bfloat16)
    grad_values = value_acc.reshape(TOKENS, KVH * HD).astype(jnp.bfloat16)
    return (grad_query, grad_keys, grad_values)
```

```python
import functools

import jax
import jax.numpy as jnp
from jax import lax
from jax.experimental import pallas as pl
from jax.experimental.pallas import tpu as pltpu
from jax.sharding import PartitionSpec as P

HD = 128
KVH = 8
GROUP = 5
BLK = 128
TOPK = 3
AXES = ("ctx", "bulk")
SCALE = HD ** (-0.5)
NT = (((1,), (1,)), ((), ()))
TN = (((0,), (0,)), ((), ()))
F32 = jnp.float32
BF16 = jnp.bfloat16


def estimate(flops, moved):
    return pl.CostEstimate(flops=flops, bytes_accessed=moved, transcendentals=0)


def stacked(ref):
    return jnp.concatenate([ref[:, g * HD : (g + 1) * HD] for g in range(GROUP)], axis=0)


def row(stat, first):
    return jnp.concatenate([stat[first + g : first + g + 1] for g in range(GROUP)], axis=1)


def item_grads(queries, grads, logs, shift, key_set, value_set, mask=None):
    scores = lax.dot_general(key_set, queries, NT, preferred_element_type=F32) * SCALE
    probs32 = jnp.exp(scores - logs)
    if mask is not None:
        probs32 = jnp.where(mask, probs32, 0.0)
    value_part = jnp.dot(probs32.astype(BF16), grads, preferred_element_type=F32)
    dprobs = lax.dot_general(value_set, grads, NT, preferred_element_type=F32)
    dscores = (probs32 * (dprobs - shift)).astype(BF16)
    key_part = jnp.dot(dscores, queries, preferred_element_type=F32) * SCALE
    return dscores, key_part, value_part


def pack_kernel(per_step, codes, keys, values, out):
    first = pl.program_id(0) * per_step

    @pl.loop(0, per_step)
    def _(i):
        code = jnp.maximum(codes[first + i], 0)
        rows = pl.ds(pl.multiple_of(code // KVH * BLK, BLK), BLK)
        cols = pl.ds(pl.multiple_of(code % KVH * HD, HD), HD)
        out[i, :, :HD] = keys[rows, cols]
        out[i, :, HD:] = values[rows, cols]


def pack(codes, keys, values):
    count = codes.shape[0]
    per_step = 8
    return pl.pallas_call(
        functools.partial(pack_kernel, per_step),
        grid_spec=pltpu.PrefetchScalarGridSpec(
            num_scalar_prefetch=1,
            grid=(count // per_step,),
            in_specs=[pl.BlockSpec(keys.shape, lambda i, c: (0, 0))] * 2,
            out_specs=pl.BlockSpec((per_step, BLK, 2 * HD), lambda i, c: (i, 0, 0)),
        ),
        out_shape=jax.ShapeDtypeStruct((count, BLK, 2 * HD), BF16),
        cost_estimate=estimate(0, count * BLK * HD * 8),
        name="pack",
    )(codes, keys, values)


def own_kernel(query, grad, output, logs, keys, values, stat, dsc, part):
    queries, grads = stacked(query), stacked(grad)
    for g in range(GROUP):
        cols = slice(g * HD, (g + 1) * HD)
        product = grad[:, cols].astype(F32) * output[:, cols].astype(F32)
        stat[0, 8 + g : 9 + g, :] = jnp.sum(product.T, axis=0, keepdims=True)
        stat[0, g : g + 1, :] = logs[0, g : g + 1, :]
    key_at = lax.broadcasted_iota(jnp.int32, (BLK, GROUP * BLK), 0)
    query_at = lax.broadcasted_iota(jnp.int32, (BLK, GROUP * BLK), 1) % BLK
    dscores, key_part, value_part = item_grads(
        queries, grads, row(stat[0], 0), row(stat[0], 8), keys[...], values[...], key_at <= query_at
    )
    dsc[0] = dscores
    part[0, :, :HD] = key_part
    part[0, :, HD:] = value_part


def own_block(query, grad_out, output, logs, keys, values):
    sets = query.shape[0] // BLK * KVH
    wide = pl.BlockSpec((BLK, GROUP * HD), lambda i: (i // KVH, i % KVH))
    narrow = pl.BlockSpec((BLK, HD), lambda i: (i // KVH, i % KVH))
    return pl.pallas_call(
        own_kernel,
        grid=(sets,),
        in_specs=[wide, wide, wide, pl.BlockSpec((1, GROUP, BLK), lambda i: (i, 0, 0)), narrow, narrow],
        out_specs=[
            pl.BlockSpec((1, 16, BLK), lambda i: (i, 0, 0)),
            pl.BlockSpec((1, BLK, GROUP * BLK), lambda i: (i, 0, 0)),
            pl.BlockSpec((1, BLK, 2 * HD), lambda i: (i, 0, 0)),
        ],
        out_shape=[
            jax.ShapeDtypeStruct((sets, 16, BLK), F32),
            jax.ShapeDtypeStruct((sets, BLK, GROUP * BLK), BF16),
            jax.ShapeDtypeStruct((sets, BLK, 2 * HD), F32),
        ],
        cost_estimate=estimate(sets * 8 * GROUP * BLK * BLK * HD, 5 * query.size * 2),
        name="own",
    )(query, grad_out, output, logs, keys, values)


def fetched_kernel(slots, query, grad, stat, item, back, dsc):
    @pl.when(slots[pl.program_id(0)] >= 0)
    def _():
        dscores, key_part, value_part = item_grads(
            stacked(query), stacked(grad), row(stat[0], 0), row(stat[0], 8), item[0, :, :HD], item[0, :, HD:]
        )
        dsc[0] = dscores
        back[0, :, :HD] = key_part.astype(BF16)
        back[0, :, HD:] = value_part.astype(BF16)


def fetched(slots, query, grad_out, stat, items, count_slots):
    count = items.shape[0]

    def at(i, s):
        return jnp.maximum(s[i], 0) // TOPK

    wide = pl.BlockSpec((BLK, GROUP * HD), lambda i, s: (at(i, s) // KVH, at(i, s) % KVH))
    return pl.pallas_call(
        fetched_kernel,
        grid_spec=pltpu.PrefetchScalarGridSpec(
            num_scalar_prefetch=1,
            grid=(count,),
            in_specs=[
                wide,
                wide,
                pl.BlockSpec((1, 16, BLK), lambda i, s: (at(i, s), 0, 0)),
                pl.BlockSpec((1, BLK, 2 * HD), lambda i, s: (i, 0, 0)),
            ],
            out_specs=[
                pl.BlockSpec((1, BLK, 2 * HD), lambda i, s: (i, 0, 0)),
                pl.BlockSpec(
                    (1, BLK, GROUP * BLK), lambda i, s: (jnp.where(s[i] >= 0, s[i], count_slots), 0, 0)
                ),
            ],
        ),
        out_shape=[
            jax.ShapeDtypeStruct((count, BLK, 2 * HD), BF16),
            jax.ShapeDtypeStruct((count_slots + 1, BLK, GROUP * BLK), BF16),
        ],
        cost_estimate=estimate(count * 8 * GROUP * BLK * BLK * HD, count * 640 * 1024),
        name="fetched",
    )(slots, query, grad_out, stat, items)


def query_kernel(owners, own_ds, keys, ds0, ds1, ds2, item0, item1, item2, out, acc):
    first = pl.program_id(0) * TOPK

    def term(ds, key_set):
        return [
            lax.dot_general(ds[:, g * BLK : (g + 1) * BLK], key_set, TN, preferred_element_type=F32)
            for g in range(GROUP)
        ]

    for g, t in enumerate(term(own_ds[0], keys[...])):
        acc[:, g * HD : (g + 1) * HD] = t
    for s, (ds, item) in enumerate(((ds0, item0), (ds1, item1), (ds2, item2))):

        @pl.when(owners[first + s] >= 0)
        def _(ds=ds, item=item):
            for g, t in enumerate(term(ds[0], item[0])):
                acc[:, g * HD : (g + 1) * HD] += t

    out[...] = (acc[...] * SCALE).astype(BF16)


def query_grads(owners, own_ds, keys, dsc, items):
    sets = own_ds.shape[0]

    def ds_at(s):
        return pl.BlockSpec((1, BLK, GROUP * BLK), lambda i, o: (i * TOPK + s, 0, 0))

    def item_at(s):
        return pl.BlockSpec((1, BLK, HD), lambda i, o: (jnp.maximum(o[i * TOPK + s], 0), 0, 0))

    return pl.pallas_call(
        query_kernel,
        grid_spec=pltpu.PrefetchScalarGridSpec(
            num_scalar_prefetch=1,
            grid=(sets,),
            in_specs=[
                pl.BlockSpec((1, BLK, GROUP * BLK), lambda i, o: (i, 0, 0)),
                pl.BlockSpec((BLK, HD), lambda i, o: (i // KVH, i % KVH)),
                ds_at(0),
                ds_at(1),
                ds_at(2),
                item_at(0),
                item_at(1),
                item_at(2),
            ],
            out_specs=pl.BlockSpec((BLK, GROUP * HD), lambda i, o: (i // KVH, i % KVH)),
            scratch_shapes=[pltpu.VMEM((BLK, GROUP * HD), F32)],
        ),
        out_shape=jax.ShapeDtypeStruct((sets // KVH * BLK, KVH * GROUP * HD), BF16),
        cost_estimate=estimate(sets * 8 * GROUP * BLK * BLK * HD, sets * 1024 * 1024),
        name="query_grads",
    )(owners, own_ds, keys, dsc, dsc, dsc, items, items, items)


def total_kernel(count, blocks, codes, part, back, out_keys, out_values, acc):
    acc[...] = part[...]

    @pl.loop(0, count)
    def _(i):
        code = codes[i]

        @pl.when(code >= 0)
        def _():
            acc[code] += back[i].astype(F32)

    for b in range(blocks):
        for h in range(KVH):
            cols = slice(h * HD, (h + 1) * HD)
            out_keys[b, :, cols] = acc[b * KVH + h, :, :HD].astype(BF16)
            out_values[b, :, cols] = acc[b * KVH + h, :, HD:].astype(BF16)


def totals(codes, part, back):
    sets, count = part.shape[0], back.shape[0]
    blocks = sets // KVH
    rows = 32
    out = jax.ShapeDtypeStruct((blocks, BLK, KVH * HD), BF16)
    out_spec = pl.BlockSpec((blocks, rows, KVH * HD), lambda i, c: (0, i, 0))
    return pl.pallas_call(
        functools.partial(total_kernel, count, blocks),
        grid_spec=pltpu.PrefetchScalarGridSpec(
            num_scalar_prefetch=1,
            grid=(BLK // rows,),
            in_specs=[
                pl.BlockSpec((sets, rows, 2 * HD), lambda i, c: (0, i, 0)),
                pl.BlockSpec((count, rows, 2 * HD), lambda i, c: (0, i, 0)),
            ],
            out_specs=[out_spec, out_spec],
            scratch_shapes=[pltpu.VMEM((sets, rows, 2 * HD), F32)],
        ),
        out_shape=[out, out],
        cost_estimate=estimate(back.size, part.size * 4 + back.size * 2),
        name="totals",
    )(codes, part, back)


def exchange(x):
    return lax.all_to_all(x, AXES, split_axis=0, concat_axis=0, tiled=True)


def shards(query, keys, values, output, grad_out, logsumexp, selected):
    count_peers = lax.axis_size(AXES)
    tok_rows = query.shape[0]
    local_blocks = tok_rows // BLK
    per_device = local_blocks * KVH * TOPK
    chosen = selected.reshape(per_device)
    owners = jnp.where(chosen >= 0, chosen // local_blocks, -1)
    slot_ids = jnp.arange(per_device, dtype=jnp.int32)
    item_code = chosen % local_blocks * KVH + slot_ids // TOPK % KVH
    peer_ids = jnp.arange(count_peers, dtype=jnp.int32)
    matches = owners[:, None] == peer_ids[None, :]
    request = jnp.max(jnp.where(matches, item_code[:, None], -1), axis=0)
    slots = jnp.max(jnp.where(matches, slot_ids[:, None], -1), axis=0)
    codes = exchange(request.reshape(count_peers, 1)).reshape(count_peers)
    arrived = exchange(pack(codes, keys, values))
    logs = jnp.transpose(logsumexp.reshape(local_blocks, BLK, KVH, GROUP), (0, 2, 3, 1))
    logs = logs.reshape(local_blocks * KVH, GROUP, BLK)
    stat, own_ds, own_part = own_block(query, grad_out, output, logs, keys, values)
    back, dsc = fetched(slots, query, grad_out, stat, arrived, per_device)
    received = exchange(back)
    grad_query = query_grads(owners, own_ds, keys, dsc, arrived)
    grad_keys, grad_values = totals(codes, own_part, received)
    return (
        grad_query,
        grad_keys.reshape(tok_rows, KVH * HD),
        grad_values.reshape(tok_rows, KVH * HD),
    )


def solution(mesh):
    rows = P(AXES, None)
    return jax.shard_map(
        shards,
        mesh=mesh,
        in_specs=(rows,) * 6 + (P(AXES, None, None),),
        out_specs=(rows,) * 3,
        check_vma=False,
    )
```

```python
import functools

import jax
import jax.numpy as jnp
from jax import lax
from jax.experimental import pallas as pl
from jax.experimental.pallas import tpu as pltpu
from jax.sharding import PartitionSpec as P


HD = 128
KVH = 8
GROUP = 5
BLK = 128
TOPK = 3
LANES = 128
AXES = ("ctx", "bulk")
SCALE = HD ** (-0.5)
NT = (((1,), (1,)), ((), ()))
TN = (((0,), (0,)), ((), ()))
F32 = jnp.float32
BF16 = jnp.bfloat16
MIB = 1024 * 1024

WHOLE = pl.BlockSpec(memory_space=pltpu.VMEM)
ANYWHERE = pl.BlockSpec(memory_space=pl.ANY)
SCALARS = pl.BlockSpec(memory_space=pltpu.SMEM)


def estimate(flops, moved):
    return pl.CostEstimate(flops=flops, bytes_accessed=moved, transcendentals=0)


def grant(mib):
    return pltpu.CompilerParams(vmem_limit_bytes=mib * MIB)


def row(stat, first):
    return jnp.concatenate([stat[first + g : first + g + 1] for g in range(GROUP)], axis=1)


def item_grads(queries, grads, stat, key_set, value_set, mask=None):
    scores = lax.dot_general(key_set, queries, NT, preferred_element_type=F32) * SCALE
    probs32 = jnp.exp(scores - row(stat, 0))
    if mask is not None:
        probs32 = jnp.where(mask, probs32, 0.0)
    value_part = jnp.dot(probs32.astype(BF16), grads, preferred_element_type=F32)
    dprobs = lax.dot_general(value_set, grads, NT, preferred_element_type=F32)
    dscores = (probs32 * (dprobs - row(stat, 8))).astype(BF16)
    key_part = jnp.dot(dscores, queries, preferred_element_type=F32) * SCALE
    return dscores, key_part, value_part


def pack_kernel(chips, place, codes, keys, values, far_keys, far_values, *outs):
    chip, core = place[0], place[1]
    for m in range(chips):
        peer = (chip ^ m) * 2 + core
        for i, (ks, vs) in enumerate(((keys, values), (far_keys, far_values))):
            code = jnp.maximum(codes[peer, core ^ i], 0)
            rows = pl.ds(pl.multiple_of((code >> 3) * BLK, BLK), BLK)
            cols = pl.ds(pl.multiple_of((code & 7) * HD, HD), HD)
            outs[m][i, :, :HD] = ks[rows, cols]
            outs[m][i, :, HD:] = vs[rows, cols]


def pack(chips, place, codes, keys, values, far_keys, far_values):
    return pl.pallas_call(
        functools.partial(pack_kernel, chips),
        in_specs=[SCALARS, SCALARS] + [WHOLE] * 4,
        out_specs=[WHOLE] * chips,
        out_shape=[jax.ShapeDtypeStruct((2, BLK, 2 * HD), BF16)] * chips,
        compiler_params=grant(16),
        cost_estimate=estimate(0, chips * BLK * HD * 16),
        name="pack",
    )(place, codes, keys, values, far_keys, far_values)


def rows_kernel(count, slots_in, query, grad, output, logs, qs, gs, stat, slots):
    at = pl.program_id(0)

    @pl.when(at == 0)
    def _():
        @pl.loop(0, count)
        def _(i):
            slots[i] = slots_in[i]

    first = lax.broadcasted_iota(jnp.int32, (BLK, BLK), 0)
    diagonal = first == lax.broadcasted_iota(jnp.int32, (BLK, BLK), 1)
    for g in range(GROUP):
        cols = slice(g * HD, (g + 1) * HD)
        rows = slice(g * BLK, (g + 1) * BLK)
        qs[at, rows, :] = query[:, cols]
        gs[at, rows, :] = grad[:, cols]
        product = lax.dot_general(output[:, cols], grad[:, cols], NT, preferred_element_type=F32)
        delta = jnp.sum(jnp.where(diagonal, product, 0.0), axis=0, keepdims=True)
        stat[at, 8 + g : 9 + g, :] = delta
        stat[at, g : g + 1, :] = logs[0, g : g + 1, :]


def query_rows(slots, query, grad_out, output, logs):
    sets = query.shape[0] // BLK * KVH
    count = slots.shape[0]
    wide = pl.BlockSpec((BLK, GROUP * HD), lambda i: (i // KVH, i % KVH))
    return pl.pallas_call(
        functools.partial(rows_kernel, count),
        grid=(sets,),
        in_specs=[SCALARS, wide, wide, wide, pl.BlockSpec((1, GROUP, BLK), lambda i: (i, 0, 0))],
        out_specs=[WHOLE] * 3 + [SCALARS],
        out_shape=[
            pltpu.VMEM((sets, GROUP * BLK, HD), BF16),
            pltpu.VMEM((sets, GROUP * BLK, HD), BF16),
            pltpu.VMEM((sets, 16, BLK), F32),
            pltpu.SMEM((count,), jnp.int32),
        ],
        compiler_params=grant(50),
        cost_estimate=estimate(sets * 2 * GROUP * BLK * BLK * HD, 4 * query.size * 2),
        name="rows",
    )(slots, query, grad_out, output, logs)


def own_kernel(qs, gs, stat, keys, values, part, dsc):
    key_at = lax.broadcasted_iota(jnp.int32, (BLK, GROUP * BLK), 0)
    query_at = lax.broadcasted_iota(jnp.int32, (BLK, GROUP * BLK), 1) % BLK

    @pl.loop(0, part.shape[0])
    def _(at):
        rows = pl.ds(pl.multiple_of((at >> 3) * BLK, BLK), BLK)
        cols = pl.ds(pl.multiple_of((at & 7) * HD, HD), HD)
        dscores, key_part, value_part = item_grads(
            qs[at], gs[at], stat[at], keys[rows, cols], values[rows, cols],
            key_at <= query_at,
        )
        dsc[at] = dscores
        part[at, :, :HD] = key_part
        part[at, :, HD:] = value_part


def own_block(qs, gs, stat, keys, values):
    sets = stat.shape[0]
    return pl.pallas_call(
        own_kernel,
        in_specs=[WHOLE] * 5,
        out_specs=[WHOLE, WHOLE],
        out_shape=[
            pltpu.VMEM((sets, BLK, 2 * HD), F32),
            pltpu.VMEM((sets, BLK, GROUP * BLK), BF16),
        ],
        compiler_params=grant(4),
        cost_estimate=estimate(sets * 8 * GROUP * BLK * BLK * HD, sets * BLK * 2 * HD * 2),
        name="own",
    )(qs, gs, stat, keys, values)


def fetched_kernel(first, slots, items, qs, gs, stat, _after, back, dsc):
    @pl.loop(0, items.shape[0])
    def _(i):
        at = slots[first + i] // TOPK

        @pl.when(slots[first + i] >= 0)
        def _():
            dscores, key_part, value_part = item_grads(
                qs[at], gs[at], stat[at], items[i, :, :HD], items[i, :, HD:]
            )
            dsc[i] = dscores
            back[i, :, :HD] = key_part.astype(BF16)
            back[i, :, HD:] = value_part.astype(BF16)


def fetched(first, slots, items, qs, gs, stat, after):
    count = items.shape[0]
    return pl.pallas_call(
        functools.partial(fetched_kernel, first),
        in_specs=[SCALARS] + [WHOLE] * 4 + [ANYWHERE],
        out_specs=[WHOLE] * 2,
        out_shape=[
            jax.ShapeDtypeStruct(items.shape, BF16),
            pltpu.VMEM((count, BLK, GROUP * BLK), BF16),
        ],
        compiler_params=grant(4),
        cost_estimate=estimate(count * 8 * GROUP * BLK * BLK * HD, count * 256 * 1024),
    )(slots, items, qs, gs, stat, after)


def query_kernel(count, slots, own_ds, keys, *rest):
    dscs, items = rest[:count], rest[count : 2 * count]
    out, done, acc = rest[2 * count :]
    sets = own_ds.shape[0]
    done[...] = jnp.zeros_like(done)

    def term(ds, key_set):
        return jnp.concatenate(
            [
                lax.dot_general(ds[:, g * BLK : (g + 1) * BLK], key_set, TN, preferred_element_type=F32)
                for g in range(GROUP)
            ],
            axis=1,
        )

    @pl.loop(0, sets)
    def _(at):
        rows = pl.ds(pl.multiple_of((at >> 3) * BLK, BLK), BLK)
        cols = pl.ds(pl.multiple_of((at & 7) * HD, HD), HD)
        acc[at] = term(own_ds[at], keys[rows, cols])

    first = 0
    for ds, item in zip(dscs, items):

        @pl.loop(0, item.shape[0])
        def _(i, ds=ds, item=item, first=first):
            at = slots[first + i] // TOPK

            @pl.when(slots[first + i] >= 0)
            def _():
                acc[at] += term(ds[i], item[i, :, :HD])

        first += item.shape[0]

    @pl.loop(0, sets)
    def _(at):
        rows = pl.ds(pl.multiple_of((at >> 3) * BLK, BLK), BLK)
        cols = pl.ds(pl.multiple_of((at & 7) * (GROUP * HD), HD), GROUP * HD)
        out[rows, cols] = (acc[at] * SCALE).astype(BF16)


def query_grads(slots, own_ds, keys, dscs, items):
    sets, count = own_ds.shape[0], len(dscs)
    return pl.pallas_call(
        functools.partial(query_kernel, count),
        in_specs=[SCALARS] + [WHOLE] * (2 + 2 * count),
        out_specs=[WHOLE, WHOLE],
        out_shape=[
            jax.ShapeDtypeStruct((sets // KVH * BLK, KVH * GROUP * HD), BF16),
            pltpu.VMEM((8, LANES), F32),
        ],
        scratch_shapes=[pltpu.VMEM((sets, BLK, GROUP * HD), F32)],
        compiler_params=grant(16),
        cost_estimate=estimate(sets * 8 * GROUP * BLK * BLK * HD, sets * 256 * 1024),
        name="query_grads",
    )(slots, own_ds, keys, *dscs, *items)


def far_pack_kernel(chips, _after, home, *rest):
    out = rest[-1]
    out[0] = home[1]
    for m in range(1, chips):
        out[m] = rest[m - 1][1]


def far_pack(after, home, backs):
    chips = len(backs) + 1
    return pl.pallas_call(
        functools.partial(far_pack_kernel, chips),
        in_specs=[ANYWHERE] + [WHOLE] * chips,
        out_specs=WHOLE,
        out_shape=jax.ShapeDtypeStruct((chips,) + home.shape[1:], BF16),
        compiler_params=grant(8),
        cost_estimate=estimate(0, chips * BLK * HD * 8),
        name="far_pack",
    )(after, home, *backs)


def near_kernel(chips, place, codes, part, *rest):
    acc = rest[-1]
    chip, core = place[0], place[1]
    acc[...] = part[...]
    for m in range(1, chips):
        code = codes[(chip ^ m) * 2 + core, core]

        @pl.when(code >= 0)
        def _():
            acc[code] += rest[m - 1][0].astype(F32)


def near_totals(chips, place, codes, part, backs):
    return pl.pallas_call(
        functools.partial(near_kernel, chips),
        in_specs=[SCALARS, SCALARS] + [WHOLE] * chips,
        out_specs=WHOLE,
        out_shape=jax.ShapeDtypeStruct(part.shape, F32),
        compiler_params=grant(16),
        cost_estimate=estimate(part.size, part.size * 8),
        name="near_totals",
    )(place, codes, part, *backs)


def far_kernel(chips, blocks, place, codes, near, far, out_keys, out_values, acc):
    chip, core = place[0], place[1]
    acc[...] = near[...]
    for m in range(chips):
        code = codes[(chip ^ m) * 2 + 1 - core, core]

        @pl.when(code >= 0)
        def _():
            acc[code] += far[m].astype(F32)

    for b in range(blocks):
        for h in range(KVH):
            rows, cols = slice(b * BLK, (b + 1) * BLK), slice(h * HD, (h + 1) * HD)
            out_keys[rows, cols] = acc[b * KVH + h, :, :HD].astype(BF16)
            out_values[rows, cols] = acc[b * KVH + h, :, HD:].astype(BF16)


def far_totals(chips, place, codes, near, far):
    blocks = near.shape[0] // KVH
    out = jax.ShapeDtypeStruct((blocks * BLK, KVH * HD), BF16)
    return pl.pallas_call(
        functools.partial(far_kernel, chips, blocks),
        in_specs=[SCALARS, SCALARS, WHOLE, WHOLE],
        out_specs=[WHOLE, WHOLE],
        out_shape=[out, out],
        scratch_shapes=[pltpu.VMEM(near.shape, F32)],
        compiler_params=grant(16),
        cost_estimate=estimate(far.size, near.size * 4 + far.size * 2),
        name="far_totals",
    )(place, codes, near, far)


def shards(query, keys, values, output, grad_out, logsumexp, selected):
    peers = lax.axis_size(AXES)
    chips = peers // 2
    tok_rows = query.shape[0]
    local_blocks = tok_rows // BLK
    per_device = local_blocks * KVH * TOPK
    here = lax.axis_index(AXES)
    chip, core = here >> 1, here & 1
    place = jnp.stack([chip, core]).astype(jnp.int32)

    def other_core(x):
        return lax.ppermute(x, AXES, [(i, i ^ 1) for i in range(peers)])

    far_keys, far_values = other_core(keys), other_core(values)

    chosen = selected.reshape(per_device)
    owners = jnp.where(chosen >= 0, chosen // local_blocks, -1)
    slot_ids = jnp.arange(per_device, dtype=jnp.int32)
    item_code = chosen % local_blocks * KVH + slot_ids // TOPK % KVH
    peer_ids = jnp.arange(peers, dtype=jnp.int32)
    lanes = jnp.arange(LANES, dtype=jnp.int32)
    asked = (peer_ids // 2 * 2)[:, None] + lanes[None, :] % 2
    request = jnp.max(
        jnp.where(owners[:, None, None] == asked[None], item_code[:, None, None], -1), axis=0
    )
    codes = lax.all_to_all(request, AXES, split_axis=0, concat_axis=0, tiled=True)
    partner = (chip ^ (peer_ids // 2)) * 2 + (core ^ (peer_ids % 2))
    slots = jnp.max(jnp.where(owners[:, None] == partner[None, :], slot_ids[:, None], -1), axis=0)

    packed = pack(chips, place, codes, keys, values, far_keys, far_values)
    logs = jnp.transpose(logsumexp.reshape(local_blocks, BLK, KVH, GROUP), (0, 2, 3, 1))
    logs = logs.reshape(local_blocks * KVH, GROUP, BLK)
    qs, gs, stat, slots = query_rows(slots, query, grad_out, output, logs)
    part, own_ds = own_block(qs, gs, stat, keys, values)

    half = chips // 2
    order = [m for k in range(half) for m in (half + k, k) if m > 0]
    items, dscs, backs = {0: packed[0]}, {}, {}
    across = {}
    for m in order:
        up = [(i, i ^ (2 * m)) for i in range(peers) if i < i ^ (2 * m)]
        across[m] = [(j, i) for i, j in up]
        items[m] = lax.ppermute(packed[m], AXES, up)
    home, dscs[0] = fetched(0, slots, packed[0], qs, gs, stat, own_ds)
    after = home
    for m in order:
        after, dscs[m] = fetched(2 * m, slots, items[m], qs, gs, stat, after)
        backs[m] = lax.ppermute(after, AXES, across[m])
    grad_query, done = query_grads(
        slots, own_ds, keys, [dscs[m] for m in range(chips)], [items[m] for m in range(chips)]
    )
    returned = [backs[m] for m in range(1, chips)]
    far = other_core(far_pack(done, home, returned))
    near = near_totals(chips, place, codes, part, returned)
    grad_keys, grad_values = far_totals(chips, place, codes, near, far)
    return grad_query, grad_keys, grad_values


def solution(mesh):
    rows = P(AXES, None)
    return jax.shard_map(
        shards,
        mesh=mesh,
        in_specs=(rows,) * 6 + (P(AXES, None, None),),
        out_specs=(rows,) * 3,
        check_vma=False,
    )
```

```python
import functools

import jax
import jax.numpy as jnp
from jax import lax
from jax.experimental import pallas as pl
from jax.experimental.pallas import tpu as pltpu
from jax.sharding import PartitionSpec as P


HD = 128
KVH = 8
GROUP = 5
BLK = 128
TOPK = 3
LANES = 128
AXES = ("ctx", "bulk")
SCALE = HD ** (-0.5)
NT = (((1,), (1,)), ((), ()))
TN = (((0,), (0,)), ((), ()))
F32 = jnp.float32
BF16 = jnp.bfloat16
MIB = 1024 * 1024

WHOLE = pl.BlockSpec(memory_space=pltpu.VMEM)
HBM = pl.BlockSpec(memory_space=pltpu.HBM)
ANYWHERE = pl.BlockSpec(memory_space=pl.ANY)
SCALARS = pl.BlockSpec(memory_space=pltpu.SMEM)


def estimate(flops, moved):
    return pl.CostEstimate(flops=flops, bytes_accessed=moved, transcendentals=0)


def grant(mib):
    return pltpu.CompilerParams(vmem_limit_bytes=mib * MIB)


def row(stat, first):
    return jnp.concatenate([stat[first + g : first + g + 1] for g in range(GROUP)], axis=1)


def item_grads(queries, grads, stat, key_set, value_set, mask=None):
    scores = lax.dot_general(key_set, queries, NT, preferred_element_type=F32) * SCALE
    probs32 = jnp.exp(scores - row(stat, 0))
    if mask is not None:
        probs32 = jnp.where(mask, probs32, 0.0)
    value_part = jnp.dot(probs32.astype(BF16), grads, preferred_element_type=F32)
    dprobs = lax.dot_general(value_set, grads, NT, preferred_element_type=F32)
    dscores = (probs32 * (dprobs - row(stat, 8))).astype(BF16)
    key_part = jnp.dot(dscores, queries, preferred_element_type=F32) * SCALE
    return dscores, key_part, value_part


def position():
    here = lax.axis_index(AXES)
    return here >> 1, here & 1


def plan_kernel(blocks, selected, keys_in, values_in, request, slots, chosen, keys, values, sem):
    chip, core = position()
    copies = [
        pltpu.make_async_copy(source, target, sem.at[n])
        for n, (source, target) in enumerate(((keys_in, keys), (values_in, values)))
    ]
    for copy in copies:
        copy.start()
    request[...] = jnp.full(request.shape, -1, jnp.int32)
    lanes = lax.broadcasted_iota(jnp.int32, (2, LANES), 1)

    @pl.loop(0, slots.shape[0])
    def _(i):
        slots[i] = -1

    for b in range(blocks):
        for h in range(KVH):
            for t in range(TOPK):
                slot = (b * KVH + h) * TOPK + t
                block = selected[t, b, h]
                chosen[slot] = block

                @pl.when(block >= 0)
                def _(slot=slot, block=block, h=h):
                    owner = lax.div(block, blocks)
                    far_chip, far_core = owner >> 1, owner & 1
                    slots[((far_chip ^ chip) << 1) + (far_core ^ core)] = slot
                    code = lax.rem(block, blocks) * KVH + h
                    rows = pl.ds(far_chip << 1, 2)
                    request[rows, :] = jnp.where(lanes == far_core, code, request[rows, :])

    for copy in copies:
        copy.wait()


def plan(peers, selected, keys, values):
    blocks = selected.shape[0]
    return pl.pallas_call(
        functools.partial(plan_kernel, blocks),
        in_specs=[SCALARS, HBM, HBM],
        out_specs=[WHOLE, SCALARS, SCALARS, WHOLE, WHOLE],
        out_shape=[
            jax.ShapeDtypeStruct((peers, LANES), jnp.int32),
            pltpu.SMEM((peers,), jnp.int32),
            pltpu.SMEM((selected.size,), jnp.int32),
            pltpu.VMEM(keys.shape, BF16),
            pltpu.VMEM(values.shape, BF16),
        ],
        scratch_shapes=[pltpu.SemaphoreType.DMA((2,))],
        compiler_params=grant(56),
        cost_estimate=estimate(0, keys.size * 4),
        name="plan",
    )(jnp.transpose(selected, (2, 0, 1)), keys, values)


def pack_kernel(chips, codes, keys, values, far_keys, far_values, wanted, *outs):
    chip, core = position()
    for m in range(chips):
        for i in range(2):
            wanted[2 * m + i] = codes[(chip ^ m) * 2 + (core ^ i), core]
        for i, (ks, vs) in enumerate(((keys, values), (far_keys, far_values))):
            code = jnp.maximum(codes[(chip ^ m) * 2 + core, core ^ i], 0)
            rows = pl.ds(pl.multiple_of((code >> 3) * BLK, BLK), BLK)
            cols = pl.ds(pl.multiple_of((code & 7) * HD, HD), HD)
            outs[m][i, :, :HD] = ks[rows, cols]
            outs[m][i, :, HD:] = vs[rows, cols]


def pack(chips, codes, keys, values, far_keys, far_values):
    wanted, *outs = pl.pallas_call(
        functools.partial(pack_kernel, chips),
        in_specs=[SCALARS] + [WHOLE] * 4,
        out_specs=[SCALARS] + [WHOLE] * chips,
        out_shape=[pltpu.SMEM((2 * chips,), jnp.int32)]
        + [jax.ShapeDtypeStruct((2, BLK, 2 * HD), BF16)] * chips,
        compiler_params=grant(4),
        cost_estimate=estimate(0, chips * BLK * HD * 16),
        name="pack",
    )(codes, keys, values, far_keys, far_values)
    return wanted, outs


def rows_kernel(pairs, chosen, query, grad, output, logs, qs, gs, stat, dsc, kbuf, outs, sems, qsem):
    sets = stat.shape[0]
    step = sets // pairs
    wide = step * GROUP * HD
    count = KVH // step

    def window(p):
        return slice(p // count * BLK, (p // count + 1) * BLK), slice(
            p % count * wide, (p % count + 1) * wide
        )

    copies = []
    for p in range(pairs):
        rows, cols = window(p)
        copies.append(
            [
                pltpu.make_async_copy(source.at[rows, cols], target.at[rows, cols], sems.at[n, p])
                for n, (source, target) in enumerate(((grad, gs), (output, outs)))
            ]
        )
        for copy in copies[-1]:
            copy.start()
    queries = pltpu.make_async_copy(query, qs, qsem)
    queries.start()

    @pl.loop(0, chosen.shape[0])
    def _(s):
        @pl.when(chosen[s] < 0)
        def _():
            dsc[s] = jnp.zeros(dsc.shape[1:], BF16)
            kbuf[s] = jnp.zeros(kbuf.shape[1:], BF16)

    first = lax.broadcasted_iota(jnp.int32, (BLK, BLK), 0)
    diagonal = first == lax.broadcasted_iota(jnp.int32, (BLK, BLK), 1)
    for p in range(pairs):
        rows, cols = window(p)
        for copy in copies[p]:
            copy.wait()
        for n in range(step * GROUP):
            at, g = p * step + n // GROUP, n % GROUP
            head = slice(cols.start + n * HD, cols.start + (n + 1) * HD)
            product = lax.dot_general(outs[rows, head], gs[rows, head], NT, preferred_element_type=F32)
            delta = jnp.sum(jnp.where(diagonal, product, 0.0), axis=0, keepdims=True)
            stat[at, 8 + g : 9 + g, :] = delta
            row_at = at % KVH * GROUP + g
            stat[at, g : g + 1, :] = logs[row_at : row_at + 1, rows]
    queries.wait()


def query_rows(chosen, query, grad_out, output, logs):
    sets = query.shape[0] // BLK * KVH
    count = chosen.shape[0]
    pairs = sets // 2
    return pl.pallas_call(
        functools.partial(rows_kernel, pairs),
        in_specs=[SCALARS, HBM, HBM, HBM, WHOLE],
        out_specs=[WHOLE] * 5,
        out_shape=[
            pltpu.VMEM(query.shape, BF16),
            pltpu.VMEM(query.shape, BF16),
            pltpu.VMEM((sets, 16, BLK), F32),
            pltpu.VMEM((count, BLK, GROUP * BLK), BF16),
            pltpu.VMEM((count, BLK, HD), BF16),
        ],
        scratch_shapes=[
            pltpu.VMEM(query.shape, BF16),
            pltpu.SemaphoreType.DMA((2, pairs)),
            pltpu.SemaphoreType.DMA,
        ],
        compiler_params=grant(40),
        cost_estimate=estimate(sets * 2 * GROUP * BLK * BLK * HD, 4 * query.size * 2),
        name="rows",
    )(chosen, query, grad_out, output, logs)


def stacked(ref, at):
    rows = pl.ds(pl.multiple_of((at >> 3) * BLK, BLK), BLK)
    first = (at & 7) * (GROUP * HD)
    return jnp.concatenate(
        [ref[rows, pl.ds(pl.multiple_of(first + g * HD, HD), HD)] for g in range(GROUP)], axis=0
    )


def fetched_kernel(m, slots, items, qs, gs, stat, _dsc, _kbuf, back, dsc, kbuf):
    @pl.loop(0, 2)
    def _(i):
        slot = slots[2 * m + i]

        @pl.when(slot >= 0)
        def _():
            at = slot // TOPK
            key_set = items[i, :, :HD]
            dscores, key_part, value_part = item_grads(
                stacked(qs, at), stacked(gs, at), stat[at], key_set, items[i, :, HD:]
            )
            dsc[slot] = dscores
            kbuf[slot] = key_set
            back[i, :, :HD] = key_part.astype(BF16)
            back[i, :, HD:] = value_part.astype(BF16)


def fetched(m, slots, items, qs, gs, stat, dsc, kbuf):
    return pl.pallas_call(
        functools.partial(fetched_kernel, m),
        in_specs=[SCALARS] + [WHOLE] * 6,
        out_specs=[WHOLE] * 3,
        out_shape=[
            jax.ShapeDtypeStruct(items.shape, BF16),
            pltpu.VMEM(dsc.shape, BF16),
            pltpu.VMEM(kbuf.shape, BF16),
        ],
        input_output_aliases={5: 1, 6: 2},
        compiler_params=grant(4),
        cost_estimate=estimate(2 * 8 * GROUP * BLK * BLK * HD, 2 * 256 * 1024),
    )(slots, items, qs, gs, stat, dsc, kbuf)


def own_kernel(qs, gs, stat, keys, values, dsc, kbuf, _after, part, out, done):
    at = pl.program_id(0)
    rows = pl.ds(pl.multiple_of((at >> 3) * BLK, BLK), BLK)
    cols = pl.ds(pl.multiple_of((at & 7) * HD, HD), HD)
    key_at = lax.broadcasted_iota(jnp.int32, (BLK, GROUP * BLK), 0)
    query_at = lax.broadcasted_iota(jnp.int32, (BLK, GROUP * BLK), 1) % BLK
    key_set = keys[rows, cols]
    dscores, key_part, value_part = item_grads(
        stacked(qs, at), stacked(gs, at), stat[at], key_set, values[rows, cols], key_at <= query_at
    )
    part[at, :, :HD] = key_part
    part[at, :, HD:] = value_part
    mine = pl.ds(at * TOPK, TOPK)
    every_ds = jnp.concatenate([dscores, dsc[mine].reshape(TOPK * BLK, GROUP * BLK)], axis=0)
    every_key = jnp.concatenate([key_set, kbuf[mine].reshape(TOPK * BLK, HD)], axis=0)
    sums = lax.dot_general(every_key, every_ds, TN, preferred_element_type=F32)
    sums = (sums * SCALE).astype(BF16)
    for g in range(GROUP):
        out[:, g * HD : (g + 1) * HD] = sums[:, g * BLK : (g + 1) * BLK].T
    done[...] = jnp.zeros_like(done)


def own_block(qs, gs, stat, keys, values, dsc, kbuf, after):
    sets = stat.shape[0]
    return pl.pallas_call(
        own_kernel,
        grid=(sets,),
        in_specs=[WHOLE] * 7 + [ANYWHERE],
        out_specs=[
            WHOLE,
            pl.BlockSpec((BLK, GROUP * HD), lambda i: (i // KVH, i % KVH)),
            WHOLE,
        ],
        out_shape=[
            pltpu.VMEM((sets, BLK, 2 * HD), F32),
            jax.ShapeDtypeStruct(qs.shape, BF16),
            pltpu.VMEM((8, LANES), F32),
        ],
        compiler_params=grant(6),
        cost_estimate=estimate(sets * 16 * GROUP * BLK * BLK * HD, qs.size * 2),
        name="own",
    )(qs, gs, stat, keys, values, dsc, kbuf, after)


def far_pack_kernel(_after, *rest):
    out = rest[-1]
    for n, back in enumerate(rest[:-1]):
        out[n] = back[1]


def far_pack(after, backs):
    return pl.pallas_call(
        far_pack_kernel,
        in_specs=[ANYWHERE] + [WHOLE] * len(backs),
        out_specs=WHOLE,
        out_shape=jax.ShapeDtypeStruct((len(backs), BLK, 2 * HD), BF16),
        compiler_params=grant(4),
        cost_estimate=estimate(0, len(backs) * BLK * HD * 8),
    )(after, *backs)


def add_back(acc, code, back):
    @pl.when(code >= 0)
    def _():
        acc[code] += back.astype(F32)


def near_kernel(order, early, wanted, part, far, *rest):
    backs, acc = rest[:-1], rest[-1]
    acc[...] = part[...]
    for m, back in zip(order, backs):
        add_back(acc, wanted[2 * m], back[0])
    for n, m in enumerate(early):
        add_back(acc, wanted[2 * m + 1], far[n])


def near_totals(order, early, wanted, part, far, backs):
    return pl.pallas_call(
        functools.partial(near_kernel, order, early),
        in_specs=[SCALARS] + [WHOLE] * (2 + len(backs)),
        out_specs=WHOLE,
        out_shape=pltpu.VMEM(part.shape, F32),
        compiler_params=grant(4),
        cost_estimate=estimate(part.size, part.size * 8),
        name="near_totals",
    )(wanted, part, far, *backs)


def far_kernel(late, wanted, near, far, out_keys, out_values, acc):
    acc[...] = near[...]
    for n, m in enumerate(late):
        add_back(acc, wanted[2 * m + 1], far[n])
    for at in range(near.shape[0]):
        b, h = at // KVH, at % KVH
        rows, cols = slice(b * BLK, (b + 1) * BLK), slice(h * HD, (h + 1) * HD)
        out_keys[rows, cols] = acc[at, :, :HD].astype(BF16)
        out_values[rows, cols] = acc[at, :, HD:].astype(BF16)


def far_totals(late, wanted, near, far):
    blocks = near.shape[0] // KVH
    out = jax.ShapeDtypeStruct((blocks * BLK, KVH * HD), BF16)
    return pl.pallas_call(
        functools.partial(far_kernel, late),
        in_specs=[SCALARS, WHOLE, WHOLE],
        out_specs=[WHOLE, WHOLE],
        out_shape=[out, out],
        scratch_shapes=[pltpu.VMEM(near.shape, F32)],
        compiler_params=grant(8),
        cost_estimate=estimate(far.size, near.size * 4 + far.size * 2),
        name="far_totals",
    )(wanted, near, far)


def shards(query, keys, values, output, grad_out, logsumexp, selected):
    peers = lax.axis_size(AXES)
    chips = peers // 2
    half = chips // 2

    def other_core(x):
        return lax.ppermute(x, AXES, [(i, i ^ 1) for i in range(peers)])

    far_keys, far_values = other_core(keys), other_core(values)
    request, slots, chosen, near_keys, near_values = plan(peers, selected, keys, values)
    codes = lax.all_to_all(request, AXES, split_axis=0, concat_axis=0, tiled=True)
    wanted, packed = pack(chips, codes, near_keys, near_values, far_keys, far_values)

    order = [m for k in range(half) for m in (half + k, k) if m > 0]
    items, backs, across = {}, {}, {}
    for m in order:
        up = [(i, i ^ (2 * m)) for i in range(peers) if i < i ^ (2 * m)]
        across[m] = [(j, i) for i, j in up]
        items[m] = lax.ppermute(packed[m], AXES, up)
    qs, gs, stat, dsc, kbuf = query_rows(chosen, query, grad_out, output, logsumexp.T)
    backs[0], dsc, kbuf = fetched(0, slots, packed[0], qs, gs, stat, dsc, kbuf)
    for m in order:
        back, dsc, kbuf = fetched(m, slots, items[m], qs, gs, stat, dsc, kbuf)
        backs[m] = lax.ppermute(back, AXES, across[m])
    early, late = [0] + order[: half - 1], order[half - 1 :]
    first = far_pack(kbuf, [backs[m] for m in early])
    part, grad_query, done = own_block(
        qs, gs, stat, near_keys, near_values, dsc, kbuf, first
    )
    first = other_core(first)
    second = other_core(far_pack(done, [backs[m] for m in late]))
    near = near_totals(order, early, wanted, part, first, [backs[m] for m in order])
    grad_keys, grad_values = far_totals(late, wanted, near, second)
    return grad_query, grad_keys, grad_values


def solution(mesh):
    rows = P(AXES, None)
    return jax.shard_map(
        shards,
        mesh=mesh,
        in_specs=(rows,) * 6 + (P(AXES, None, None),),
        out_specs=(rows,) * 3,
        check_vma=False,
    )
```
